32 devices in a mesh: gx: 4 (over x, core), gy: 4 (over z), gz: 2 (over y).
Axes of the slice: x: 2, y: 2, z: 4, core: 2. Of those that a mesh axis runs over, the one named last changes fastest.
Arguments:
- loads: bfloat16 [4, 4, 2, 2048, 128], P('gx', 'gy', 'gz'), may hold values from -12 to 12, as said below
- start_guess: bfloat16 [4, 4, 2, 2048, 128], P('gx', 'gy', 'gz'), may hold values from -1.1953125 to 1.1953125
- schur_blocks: bfloat16 [4, 4, 2, 2048, 2048], P('gx', 'gy', 'gz'), may hold values from -1 to 5, as said below
- coupling: bfloat16 [4, 4, 2, 6, 128, 128], P('gx', 'gy', 'gz'), may hold values from -0.25 to 0.25
- diag_inverse: bfloat16 [4, 4, 2, 16, 128, 128], P('gx', 'gy', 'gz'), may hold values from -1 to 1, as said below
- lower_blocks: bfloat16 [4, 4, 2, 15, 128, 128], P('gx', 'gy', 'gz'), may hold values from -0.1875 to 0.1875
- upper_blocks: bfloat16 [4, 4, 2, 15, 128, 128], P('gx', 'gy', 'gz'), may hold values from -0.1875 to 0.1875
Outputs:
- solution: float32 [4, 4, 2, 2048, 128], P('gx', 'gy', 'gz')
- residual_ratio: float32 [128], replicated
The draws below stay inside these ranges and needn't reach their ends.
Inputs may be any that keep to these rules, and one draw needn't show every extreme that they name: Each subdomain's loads are independent entries times a factor of that subdomain. `schur_blocks`: each subdomain's Schur block has a positive diagonal between 2 and 4 and full independent off-diagonal entries. `diag_inverse`: each block has a positive diagonal between 0.25 and 0.5 and full independent off-diagonal entries.
All inputs are finite; a program needn't handle non-finite values.
Results may differ from the reference program's by a relative error of at most 0.0037.
Values may be sent and summed in bfloat16 or wider, within the bound.
A program may use at most 64 MiB of HBM per device.

```python
import math
import jax
import jax.numpy as jnp
from jax import lax

U = 2048
F = 128
B = 128
R = 128
ITERS = 2
NB = 16
SX = 4
SY = 4
SZ = 2


def draw_loads(key, part):
    key_scale, key_values = jax.random.split(jax.random.fold_in(key, 11))
    scales = jnp.exp(jax.random.uniform(key_scale, (SX, SY, SZ, 1, 1), jnp.float32, math.log(0.3), math.log(3.0)))
    values = jnp.clip(jax.random.normal(key_values, (SX, SY, SZ, U, R), jnp.float32), -4.0, 4.0)
    return (values * scales).astype(jnp.bfloat16)


def draw_schur_blocks(key, part):
    key_diag, key_rest = jax.random.split(jax.random.fold_in(key, 23))
    diagonal = jnp.exp(jax.random.uniform(key_diag, (SX, SY, SZ, U), jnp.float32, math.log(2.0), math.log(4.0)))
    off_diagonal = jnp.clip(jax.random.normal(key_rest, (SX, SY, SZ, U, U), jnp.float32), -4.0, 4.0)
    matrix = off_diagonal * (0.6 / math.sqrt(U)) + diagonal[..., None] * jnp.eye(U, dtype=jnp.float32)
    return matrix.astype(jnp.bfloat16)


def draw_diag_inverse(key, part):
    key_diag, key_rest = jax.random.split(jax.random.fold_in(key, 37))
    diagonal = jnp.exp(jax.random.uniform(key_diag, (SX, SY, SZ, NB, B), jnp.float32, math.log(0.25), math.log(0.5)))
    off_diagonal = jnp.clip(jax.random.normal(key_rest, (SX, SY, SZ, NB, B, B), jnp.float32), -4.0, 4.0)
    matrix = off_diagonal * (0.1 / math.sqrt(B)) + diagonal[..., None] * jnp.eye(B, dtype=jnp.float32)
    return matrix.astype(jnp.bfloat16)


def levels(rng, dims, cuts, smallest, high):
    def one(position, parts):
        draws = jax.random.uniform(jax.random.fold_in(jax.random.fold_in(rng, 6), position), (parts,), jnp.float32, smallest / len(cuts), high / len(cuts))
        return jnp.repeat(jnp.exp(draws), dims[position] // parts).reshape((-1,) + (1,) * (len(dims) - position - 1))

    gain = one(*cuts[0])
    for cut in cuts[1:]:
        gain = gain * one(*cut)
    return gain


def normal_values(key, shape, scale, limit, cuts=(), held_as=jnp.bfloat16):
    values = jax.random.normal(key, shape, jnp.float32) * scale
    if len(cuts) > 0:
        values = levels(key, shape, cuts, -0.22, 0.18) * values
    return jnp.clip(values, min=-limit, max=limit).astype(held_as)


def setup_inputs(seed: int = 0) -> dict:
    arg_keys = jax.random.split(jax.random.key(seed), 8)
    return {
        "loads": draw_loads(jax.random.fold_in(arg_keys[7], 71), 0),
        "start_guess": normal_values(arg_keys[1], (SX, SY, SZ, U, R), 0.3, 1.1953125, ((0, 4), (1, 4), (2, 2))),
        "schur_blocks": draw_schur_blocks(jax.random.fold_in(arg_keys[7], 71), 0),
        "coupling": normal_values(arg_keys[3], (SX, SY, SZ, 6, F, F), (4 * F) ** -0.5, 0.25, ((0, 4), (1, 4), (2, 2))),
        "diag_inverse": draw_diag_inverse(jax.random.fold_in(arg_keys[7], 71), 0),
        "lower_blocks": normal_values(arg_keys[5], (SX, SY, SZ, NB - 1, B, B), (9 * B) ** -0.5, 0.1875, ((0, 4), (1, 4), (2, 2))),
        "upper_blocks": normal_values(arg_keys[6], (SX, SY, SZ, NB - 1, B, B), (9 * B) ** -0.5, 0.1875, ((0, 4), (1, 4), (2, 2))),
    }


epsilon = 1e-06

def operate(values, schur_blocks, coupling):
    shape = values.shape
    total = shape[0] * shape[1] * shape[2]
    face_rows = values[..., :6 * F, :].reshape(shape[:3] + (6, F, shape[4]))
    neighbours = jnp.stack([jnp.roll(face_rows[:, :, :, 1], 1, 0), jnp.roll(face_rows[:, :, :, 0], -1, 0), jnp.roll(face_rows[:, :, :, 3], 1, 1), jnp.roll(face_rows[:, :, :, 2], -1, 1), jnp.roll(face_rows[:, :, :, 5], 1, 2), jnp.roll(face_rows[:, :, :, 4], -1, 2)], axis=3)

    def single(inputs):
        schur_block, vector_in, couple_block, beside_all = inputs
        own_part = jnp.dot(schur_block, vector_in, preferred_element_type=jnp.float32)
        coupled = jnp.einsum('fgk,fkr->fgr', couple_block.astype(jnp.float32), beside_all.astype(jnp.float32), precision=lax.Precision.HIGHEST)
        return jnp.concatenate([own_part[:6 * F] + coupled.reshape(6 * F, R), own_part[6 * F:]], axis=0)
    result = lax.map(single, (schur_blocks.reshape(total, U, U), values.reshape(total, U, R), coupling.reshape(total, 6, F, F), neighbours.reshape(total, 6, F, R)))
    return result.reshape(shape[:3] + (U, R))

def apply_block(matrix, vector):
    rounded = lax.optimization_barrier(vector.astype(jnp.bfloat16))
    return jnp.einsum('xyzij,xyzjr->xyzir', matrix.astype(jnp.float32), rounded.astype(jnp.float32), precision=lax.Precision.HIGHEST)

def precondition(values, diag_inverse, lower_blocks, upper_blocks):
    shape = values.shape
    blocks = values.reshape(shape[:3] + (NB, B, R))
    forward_sweep = [blocks[:, :, :, 0]]
    for number in range(1, NB):
        forward_sweep.append(blocks[:, :, :, number] - apply_block(lower_blocks[:, :, :, number - 1], forward_sweep[-1]))
    result = [None] * NB
    result[NB - 1] = apply_block(diag_inverse[:, :, :, NB - 1], forward_sweep[NB - 1])
    for number in range(NB - 2, -1, -1):
        inner = forward_sweep[number] - apply_block(upper_blocks[:, :, :, number], result[number + 1])
        result[number] = apply_block(diag_inverse[:, :, :, number], inner)
    return jnp.stack(result, axis=3).reshape(shape)

def least_squares(hessenberg, start_norm):
    columns = hessenberg.shape[1]
    unit_vectors = []
    triangle = {}
    for column in range(columns):
        vector = hessenberg[:, column]
        for earlier in range(column):
            weight = lax.optimization_barrier(jnp.sum(unit_vectors[earlier] * vector, axis=0))
            triangle[earlier, column] = weight
            vector = vector - weight * unit_vectors[earlier]
        length = jnp.sqrt(lax.optimization_barrier(jnp.sum(vector * vector, axis=0)))
        triangle[column, column] = length
        unit_vectors.append(vector / length)
    target = [start_norm * unit_vectors[column][0] for column in range(columns)]
    coeffs = [None] * columns
    for column in range(columns - 1, -1, -1):
        running = target[column]
        for earlier in range(column + 1, columns):
            running = running - triangle[column, earlier] * coeffs[earlier]
        coeffs[column] = running / triangle[column, column]
    coeffs = jnp.stack(coeffs)
    unit_first = jnp.zeros((columns + 1, 1), jnp.float32).at[0].set(1.0)
    misfit = unit_first * start_norm - lax.optimization_barrier(jnp.sum(hessenberg * coeffs[None], axis=1))
    return (coeffs, jnp.sqrt(lax.optimization_barrier(jnp.sum(misfit * misfit, axis=0))) / start_norm)

def reference(loads, start_guess, schur_blocks, coupling, diag_inverse, lower_blocks, upper_blocks):
    residual = loads.astype(jnp.float32) - operate(start_guess, schur_blocks, coupling)
    start_norm = jnp.sqrt(lax.optimization_barrier(jnp.sum(residual * residual, axis=(0, 1, 2, 3))) + epsilon)
    krylov = [residual / start_norm]
    hessenberg = jnp.zeros((ITERS + 1, ITERS, R), jnp.float32)
    directions = []
    for column in range(ITERS):
        direction = precondition(krylov[column], diag_inverse, lower_blocks, upper_blocks)
        directions.append(direction)
        rounded = lax.optimization_barrier(direction.astype(jnp.bfloat16))
        mapped = operate(rounded, schur_blocks, coupling)
        stacked = jnp.stack(krylov)
        projected = lax.optimization_barrier(jnp.sum(stacked * mapped[None], axis=(1, 2, 3, 4)))
        mapped = mapped - lax.optimization_barrier(jnp.sum(projected[:, None, None, None, None, :] * stacked, axis=0))
        length = jnp.sqrt(lax.optimization_barrier(jnp.sum(mapped * mapped, axis=(0, 1, 2, 3))) + epsilon)
        hessenberg = hessenberg.at[:column + 1, column].set(projected).at[column + 1, column].set(length)
        if column + 1 < ITERS:
            krylov.append(mapped / length)
    coeffs, residual_ratio = least_squares(hessenberg, start_norm)
    solution = start_guess.astype(jnp.float32)
    for column in range(ITERS):
        solution = solution + coeffs[column] * directions[column]
    return (solution, residual_ratio)
```

```python
import functools

import jax
import jax.numpy as jnp
from jax import lax
from jax.experimental import pallas as pl
from jax.experimental.pallas import tpu as pltpu
from jax.sharding import PartitionSpec as P

AXES = ("gx", "gy", "gz")
MESH = pl.DeviceIdType.MESH
EPS = 1e-06
GROUP = 4
bf16 = jnp.bfloat16
f32 = jnp.float32


def dot(a, b):
    return jnp.dot(a, b, preferred_element_type=f32)


def split(v):
    hi = v.astype(bf16)
    lo = (v - hi.astype(f32)).astype(bf16)
    return jnp.concatenate([hi, lo], axis=1)


def fold(y):
    r = y.shape[1] // 2
    return y[:, :r] + y[:, r:]


def colsum(v):
    return jnp.sum(v, axis=0, keepdims=True)


def least_squares(h, start_norm):
    t00 = jnp.sqrt(h[0][0] * h[0][0] + h[1][0] * h[1][0])
    q0 = [h[0][0] / t00, h[1][0] / t00]
    t01 = q0[0] * h[0][1] + q0[1] * h[1][1]
    v1 = [h[0][1] - t01 * q0[0], h[1][1] - t01 * q0[1], h[2][1]]
    t11 = jnp.sqrt(v1[0] * v1[0] + v1[1] * v1[1] + v1[2] * v1[2])
    c1 = start_norm * (v1[0] / t11) / t11
    c0 = (start_norm * q0[0] - t01 * c1) / t00
    e0 = start_norm - h[0][0] * c0 - h[0][1] * c1
    e1 = h[1][0] * c0 + h[1][1] * c1
    e2 = h[2][1] * c1
    return c0, c1, jnp.sqrt(e0 * e0 + e1 * e1 + e2 * e2) / start_norm


def kernel(
    sizes, phases, b_hbm, x_hbm, s_hbm, c_hbm, d_hbm, l_hbm, u_hbm,
    d1_hbm, d2_hbm, coef_ref, ratio_ref,
    s_v, c_v, d_v, l_v, u_v, b_v, x_v,
    t_v, cf_v, e_v, z_v, cb_v,
    r0_v, m1_v, w_v, wcat_v, d1_v, d2_v, xcat_v,
    nb0_v, nb1_v, nb2_v, sum_bufs,
    s_sem, in_sem, out_sem, send_sem, recv_sem, sum_send, sum_recv,
):
    nb, blk = d_v.shape[0], d_v.shape[1]
    rhs = b_v.shape[1]
    unknowns = b_v.shape[0]
    faces = c_v.shape[0]
    fr = faces * blk
    groups = nb // GROUP
    chunks = s_sem.shape[0]
    rows = unknowns // chunks
    me = {a: lax.axis_index(a) for a in AXES}

    loads = [
        pltpu.make_async_copy(l_hbm, l_v, in_sem.at[0]),
        pltpu.make_async_copy(x_hbm, x_v, in_sem.at[1]),
        pltpu.make_async_copy(u_hbm, u_v, in_sem.at[2]),
        pltpu.make_async_copy(d_hbm, d_v, in_sem.at[3]),
    ]
    s_loads = [
        pltpu.make_async_copy(
            s_hbm.at[pl.ds(i * rows, rows)], s_v.at[pl.ds(i * rows, rows)], s_sem.at[i]
        )
        for i in range(chunks)
    ]
    late = [
        pltpu.make_async_copy(b_hbm, b_v, in_sem.at[4]),
        pltpu.make_async_copy(c_hbm, c_v, in_sem.at[5]),
    ]
    for c in loads + s_loads + late:
        c.start()

    def peer_of(names, k):
        index, count = 0, 1
        for a in names:
            index = index * sizes[a] + me[a]
            count = count * sizes[a]
        other = lax.rem(index + k, count)
        ids, left = {}, other
        for a in reversed(names):
            ids[a] = lax.rem(left, sizes[a])
            left = left // sizes[a]
        return index, other, count, ids

    barrier = pltpu.get_barrier_semaphore()
    greeted = 0
    for names in phases:
        count = 1
        for a in names:
            count *= sizes[a]
        for k in range(1, count):
            pl.semaphore_signal(
                barrier, inc=1, device_id=peer_of(names, k)[3], device_id_type=MESH
            )
            greeted += 1

    def halo(src, dst, stage):
        copies = []
        for f in range(faces):
            a = AXES[f // 2]
            step = 1 if f % 2 else sizes[a] - 1
            copies.append(
                pltpu.make_async_remote_copy(
                    src_ref=src.at[pl.ds(f * blk, blk)],
                    dst_ref=dst.at[f ^ 1],
                    send_sem=send_sem.at[stage, f],
                    recv_sem=recv_sem.at[stage, f ^ 1],
                    device_id={a: lax.rem(me[a] + step, sizes[a])},
                    device_id_type=MESH,
                )
            )
        for c in copies:
            c.start()
        return copies

    loads[0].wait()
    for g in range(groups):
        a = g * GROUP
        for i in range(1, GROUP):
            t_v[g, pl.ds(i * blk, blk), pl.ds((i - 1) * blk, blk)] = -l_v[a + i - 1]
        for i in range(2, GROUP):
            width = (i - 1) * blk
            before = t_v[g, pl.ds((i - 1) * blk, blk), pl.ds(0, width)]
            t_v[g, pl.ds(i * blk, blk), pl.ds(0, width)] = (
                -dot(l_v[a + i - 1], before)
            ).astype(bf16)
        if g > 0:
            carry = -l_v[a - 1]
            cf_v[g, pl.ds(0, blk)] = carry
            for i in range(1, GROUP):
                carry = (-dot(l_v[a + i - 1], carry)).astype(bf16)
                cf_v[g, pl.ds(i * blk, blk)] = carry

    pl.semaphore_wait(barrier, greeted)
    first = halo(x_hbm, nb0_v, 0)

    loads[2].wait()
    loads[3].wait()
    for k in range(nb - 1):
        e_v[k] = (-dot(d_v[k], u_v[k])).astype(bf16)
    for g in range(groups):
        a = g * GROUP
        for i in range(GROUP - 1, -1, -1):
            z_v[g, pl.ds(i * blk, blk), pl.ds(i * blk, blk)] = d_v[a + i]
            if i < GROUP - 1:
                width = (GROUP - 1 - i) * blk
                after = z_v[g, pl.ds((i + 1) * blk, blk), pl.ds((i + 1) * blk, width)]
                z_v[g, pl.ds(i * blk, blk), pl.ds((i + 1) * blk, width)] = dot(
                    e_v[a + i], after
                ).astype(bf16)
        if g < groups - 1:
            carry = e_v[a + GROUP - 1]
            cb_v[g, pl.ds((GROUP - 1) * blk, blk)] = carry
            for i in range(GROUP - 2, -1, -1):
                carry = dot(e_v[a + i], carry).astype(bf16)
                cb_v[g, pl.ds(i * blk, blk)] = carry

    loads[1].wait()
    for i in range(chunks):
        s_loads[i].wait()
        r0_v[pl.ds(i * rows, rows)] = -dot(s_v[pl.ds(i * rows, rows)], x_v[...])
    late[0].wait()
    late[1].wait()
    g00 = jnp.zeros((1, rhs), f32)
    for i in range(nb - 1, -1, -1):
        here = pl.ds(i * blk, blk)
        r = r0_v[here] + b_v[here].astype(f32)
        if i < faces:
            first[i ^ 1].wait_recv()
            r = r - dot(c_v[i], nb0_v[i])
        r0_v[here] = r
        g00 = g00 + colsum(r * r)

    def precondition(v_v, z_out):
        gs = GROUP * blk
        last = None
        for g in range(groups):
            rows_g = pl.ds(g * gs, gs)
            cat = split(v_v[rows_g])
            parts = [v_v[pl.ds(g * gs, blk)]]
            for i in range(1, GROUP):
                parts.append(
                    v_v[pl.ds(g * gs + i * blk, blk)]
                    + fold(dot(t_v[g, pl.ds(i * blk, blk), pl.ds(0, i * blk)], cat[: i * blk]))
                )
            w_v[rows_g] = jnp.concatenate(parts, axis=0)
        for g in range(groups):
            rows_g = pl.ds(g * gs, gs)
            w = w_v[rows_g]
            if g > 0:
                w = w + fold(dot(cf_v[g], last))
            cat = split(w)
            wcat_v[rows_g] = cat
            last = cat[gs - blk :]
        for g in range(groups):
            for i in range(GROUP):
                here = pl.ds(g * gs + i * blk, blk)
                rest = (GROUP - i) * blk
                z_out[here] = fold(
                    dot(
                        z_v[g, pl.ds(i * blk, blk), pl.ds(i * blk, rest)],
                        wcat_v[pl.ds(g * gs + i * blk, rest)],
                    )
                )
        for g in range(groups - 2, -1, -1):
            head = split(z_out[pl.ds((g + 1) * gs, blk)])
            rows_g = pl.ds(g * gs, gs)
            z_out[rows_g] = z_out[rows_g] + fold(dot(cb_v[g], head))

    precondition(r0_v, d1_v)
    for i in range(nb):
        here = pl.ds(i * blk, blk)
        xcat_v[0, here] = split(d1_v[here])
    second = halo(xcat_v.at[0], nb1_v, 1)
    d1_out = pltpu.make_async_copy(d1_v, d1_hbm, out_sem.at[0])
    d1_out.start()
    m1_v[pl.ds(fr, unknowns - fr)] = (
        fold(dot(s_v[pl.ds(fr, unknowns - fr)], xcat_v[0])) - r0_v[pl.ds(fr, unknowns - fr)]
    )
    m1_v[pl.ds(0, fr)] = fold(dot(s_v[pl.ds(0, fr)], xcat_v[0])) - r0_v[pl.ds(0, fr)]
    g01 = jnp.zeros((1, rhs), f32)
    g11 = jnp.zeros((1, rhs), f32)
    for i in range(nb - 1, -1, -1):
        here = pl.ds(i * blk, blk)
        m = m1_v[here]
        if i < faces:
            second[i ^ 1].wait_recv()
            m = m + fold(dot(c_v[i], nb1_v[i]))
            m1_v[here] = m
        g01 = g01 + colsum(m * r0_v[here])
        g11 = g11 + colsum(m * m)

    precondition(m1_v, d2_v)
    for i in range(nb):
        here = pl.ds(i * blk, blk)
        x_v[here] = d2_v[here].astype(bf16)
    third = halo(x_v, nb2_v, 2)
    d2_out = pltpu.make_async_copy(d2_v, d2_hbm, out_sem.at[1])
    d2_out.start()
    w_v[pl.ds(fr, unknowns - fr)] = dot(s_v[pl.ds(fr, unknowns - fr)], x_v[...])
    w_v[pl.ds(0, fr)] = dot(s_v[pl.ds(0, fr)], x_v[...])
    g02 = jnp.zeros((1, rhs), f32)
    g12 = jnp.zeros((1, rhs), f32)
    g22 = jnp.zeros((1, rhs), f32)
    for i in range(nb - 1, -1, -1):
        here = pl.ds(i * blk, blk)
        m = w_v[here]
        if i < faces:
            third[i ^ 1].wait_recv()
            m = m + dot(c_v[i], nb2_v[i])
        g02 = g02 + colsum(m * r0_v[here])
        g12 = g12 + colsum(m * m1_v[here])
        g22 = g22 + colsum(m * m)

    zero = jnp.zeros((1, rhs), f32)
    total = jnp.concatenate([g00, g01, g11, g02, g12, g22, zero, zero], axis=0)
    base = 0
    for p, names in enumerate(phases):
        buf = sum_bufs[p]
        index, _, count, _ = peer_of(names, 0)
        buf[index] = total
        copies = []
        for k in range(1, count):
            ids = peer_of(names, k)[3]
            copies.append(
                pltpu.make_async_remote_copy(
                    src_ref=buf.at[index],
                    dst_ref=buf.at[index],
                    send_sem=sum_send.at[base + k],
                    recv_sem=sum_recv.at[base + index],
                    device_id=ids,
                    device_id_type=MESH,
                )
            )
        for c in copies:
            c.start()
        for k in range(1, count):
            other = peer_of(names, k)[1]
            pltpu.make_async_copy(
                buf.at[other], buf.at[other], sum_recv.at[base + other]
            ).wait()
        total = buf[0]
        for k in range(1, count):
            total = total + buf[k]
        for c in copies:
            c.wait_send()
        base += count

    g00, g01, g11, g02, g12, g22 = [total[i : i + 1] for i in range(6)]
    b2 = g00 + EPS
    start = jnp.sqrt(b2)
    h00 = (g01 + g00) / b2
    de = h00 - 1.0
    n1 = (g11 - 2.0 * de * g01 + de * de * g00) / b2
    h10 = jnp.sqrt(jnp.maximum(n1, 0.0) + EPS)
    s2 = start * h10
    r0q = g02 - de * (g01 + g00)
    m1q = g12 - de * (g11 + g01)
    h01 = r0q / (start * s2)
    h11 = (m1q - de * r0q) / (s2 * s2)
    qq = (
        g22 - 2.0 * de * (g12 + g02) + de * de * (g11 + 2.0 * g01 + g00)
    ) / (s2 * s2)
    k00 = g00 / b2
    k11 = n1 / (h10 * h10)
    k01 = (g01 - de * g00) / (start * s2)
    n2 = qq - 2.0 * (h01 * h01 + h11 * h11) + h01 * h01 * k00 + h11 * h11 * k11
    n2 = n2 + 2.0 * h01 * h11 * k01
    h21 = jnp.sqrt(jnp.maximum(n2, 0.0) + EPS)
    c0, c1, ratio = least_squares([[h00, h01], [h10, h11], [zero, h21]], start)
    a2 = c1 / s2
    coef_ref[...] = jnp.concatenate([c0 / start - de * a2, a2], axis=0)
    ratio_ref[...] = ratio
    for c in first + second + third:
        c.wait_send()
    d1_out.wait()
    d2_out.wait()


def body(sizes, loads, start_guess, schur, coupling, diag_inverse, lower, upper):
    b, x, s, c, d, l, u = [
        v.reshape(v.shape[3:])
        for v in (loads, start_guess, schur, coupling, diag_inverse, lower, upper)
    ]
    n, r = b.shape
    nb, blk = d.shape[:2]
    faces = c.shape[0]
    groups = nb // GROUP
    gs = GROUP * blk
    chunks = 4
    phases = (("gx",), ("gy", "gz"))
    if sizes["gy"] * sizes["gz"] > 32:
        phases = (("gx",), ("gy",), ("gz",))
    counts = []
    for names in phases:
        count = 1
        for a in names:
            count *= sizes[a]
        counts.append(count)
    any_spec = pl.BlockSpec(memory_space=pl.ANY)
    vmem = pl.BlockSpec(memory_space=pltpu.VMEM)
    d1, d2, coef, ratio = pl.pallas_call(
        functools.partial(kernel, sizes, phases),
        out_shape=(
            jax.ShapeDtypeStruct((n, r), f32),
            jax.ShapeDtypeStruct((n, r), f32),
            jax.ShapeDtypeStruct((2, r), f32),
            jax.ShapeDtypeStruct((1, r), f32),
        ),
        in_specs=[any_spec] * 7,
        out_specs=(any_spec, any_spec, vmem, vmem),
        scratch_shapes=[
            pltpu.VMEM(s.shape, bf16),
            pltpu.VMEM(c.shape, bf16),
            pltpu.VMEM(d.shape, bf16),
            pltpu.VMEM(l.shape, bf16),
            pltpu.VMEM(u.shape, bf16),
            pltpu.VMEM((n, r), bf16),
            pltpu.VMEM((n, r), bf16),
            pltpu.VMEM((groups, gs, gs), bf16),
            pltpu.VMEM((groups, gs, blk), bf16),
            pltpu.VMEM((nb - 1, blk, blk), bf16),
            pltpu.VMEM((groups, gs, gs), bf16),
            pltpu.VMEM((groups, gs, blk), bf16),
            pltpu.VMEM((n, r), f32),
            pltpu.VMEM((n, r), f32),
            pltpu.VMEM((n, r), f32),
            pltpu.VMEM((n, 2 * r), bf16),
            pltpu.VMEM((n, r), f32),
            pltpu.VMEM((n, r), f32),
            pltpu.VMEM((1, n, 2 * r), bf16),
            pltpu.VMEM((faces, blk, r), bf16),
            pltpu.VMEM((faces, blk, 2 * r), bf16),
            pltpu.VMEM((faces, blk, r), bf16),
            [pltpu.VMEM((count, 8, r), f32) for count in counts],
            pltpu.SemaphoreType.DMA((chunks,)),
            pltpu.SemaphoreType.DMA((6,)),
            pltpu.SemaphoreType.DMA((2,)),
            pltpu.SemaphoreType.DMA((3, faces)),
            pltpu.SemaphoreType.DMA((3, faces)),
            pltpu.SemaphoreType.DMA((sum(counts),)),
            pltpu.SemaphoreType.DMA((sum(counts),)),
        ],
        compiler_params=pltpu.CompilerParams(collective_id=0, has_side_effects=True),
    )(b, x, s, c, d, l, u)
    out = x.astype(f32) + coef[0:1] * d1 + coef[1:2] * d2
    return out[None, None, None], ratio.reshape(r)


def solution(mesh):
    sizes = {a: mesh.shape[a] for a in AXES}
    deep = P("gx", "gy", "gz", None, None, None)
    flat = P("gx", "gy", "gz", None, None)
    return jax.shard_map(
        functools.partial(body, sizes),
        mesh=mesh,
        in_specs=(flat, flat, flat, deep, deep, deep, deep),
        out_specs=(flat, P()),
        check_vma=False,
    )
```

```python
import functools
import itertools
import math

import jax
import jax.numpy as jnp
from jax import lax
from jax.experimental import pallas as pl
from jax.experimental.pallas import tpu as pltpu
from jax.sharding import PartitionSpec as P

AXES = ("gx", "gy", "gz")
MESH = pl.DeviceIdType.MESH
EPS = 1e-06
GROUP = 4
bf16 = jnp.bfloat16
f32 = jnp.float32


def dot(a, b):
    return jnp.dot(a, b, preferred_element_type=f32)


def split(v):
    hi = v.astype(bf16)
    lo = (v - hi.astype(f32)).astype(bf16)
    return jnp.concatenate([hi, lo], axis=1)


def fold(y):
    r = y.shape[1] // 2
    return y[:, :r] + y[:, r:]


def colsum(v):
    return jnp.sum(v, axis=0, keepdims=True)


def least_squares(h, start_norm):
    t00 = jnp.sqrt(h[0][0] * h[0][0] + h[1][0] * h[1][0])
    q0 = [h[0][0] / t00, h[1][0] / t00]
    t01 = q0[0] * h[0][1] + q0[1] * h[1][1]
    v1 = [h[0][1] - t01 * q0[0], h[1][1] - t01 * q0[1], h[2][1]]
    t11 = jnp.sqrt(v1[0] * v1[0] + v1[1] * v1[1] + v1[2] * v1[2])
    c1 = start_norm * (v1[0] / t11) / t11
    c0 = (start_norm * q0[0] - t01 * c1) / t00
    e0 = start_norm - h[0][0] * c0 - h[0][1] * c1
    e1 = h[1][0] * c0 + h[1][1] * c1
    e2 = h[2][1] * c1
    return c0, c1, jnp.sqrt(e0 * e0 + e1 * e1 + e2 * e2) / start_norm


def kernel(
    sizes, phases, b_hbm, x_hbm, s_hbm, c_hbm, d_hbm, l_hbm, u_hbm,
    x_v, d1_v, d2_v, coef_ref, ratio_ref,
    s_v, c_v, d_v, l_v, u_v, b_v, xd_v,
    t_v, cf_v, e_v, z_v, cb_v,
    r0_v, m1_v, w_v, wcat_v, xcat_v, face_v,
    nb0_v, nb1_v, nb2_v, sum_bufs,
    s_sem, in_sem, send_sem, recv_sem, sum_send, sum_recv,
):
    nb, blk = d_v.shape[0], d_v.shape[1]
    rhs = b_v.shape[1]
    unknowns = b_v.shape[0]
    faces = c_v.shape[0]
    fr = faces * blk
    groups = nb // GROUP
    chunks = s_sem.shape[0]
    rows = unknowns // chunks
    me = {a: lax.axis_index(a) for a in AXES}

    loads = [
        pltpu.make_async_copy(l_hbm, l_v, in_sem.at[0]),
        pltpu.make_async_copy(x_hbm, x_v, in_sem.at[1]),
        pltpu.make_async_copy(u_hbm, u_v, in_sem.at[2]),
        pltpu.make_async_copy(d_hbm, d_v, in_sem.at[3]),
    ]
    s_loads = [
        pltpu.make_async_copy(
            s_hbm.at[pl.ds(i * rows, rows)], s_v.at[pl.ds(i * rows, rows)], s_sem.at[i]
        )
        for i in range(chunks)
    ]
    late = [
        pltpu.make_async_copy(b_hbm, b_v, in_sem.at[4]),
        pltpu.make_async_copy(c_hbm, c_v, in_sem.at[5]),
    ]
    for c in loads + s_loads + late:
        c.start()

    away = {
        a: [me[a]] + [lax.rem(me[a] + k, sizes[a]) for k in range(1, sizes[a])] for a in AXES
    }

    def place(names, ids):
        index = 0
        for a in names:
            index = index * sizes[a] + ids[a]
        return index

    def peers(names):
        steps = itertools.product(*[range(sizes[a]) for a in names])
        return [
            {a: away[a][k] for a, k in zip(names, step)} for step in steps if any(step)
        ]

    barrier = pltpu.get_barrier_semaphore()
    greeted = 0
    for names in phases:
        for ids in peers(names):
            pl.semaphore_signal(barrier, inc=1, device_id=ids, device_id_type=MESH)
            greeted += 1

    def face_copy(src, dst, stage, f):
        a = AXES[f // 2]
        step = 1 if f % 2 else sizes[a] - 1
        return pltpu.make_async_remote_copy(
            src_ref=src,
            dst_ref=dst.at[f ^ 1],
            send_sem=send_sem.at[stage, f],
            recv_sem=recv_sem.at[stage, f ^ 1],
            device_id={a: lax.rem(me[a] + step, sizes[a])},
            device_id_type=MESH,
        )

    loads[0].wait()
    for g in range(groups):
        a = g * GROUP
        for i in range(1, GROUP):
            t_v[g, pl.ds(i * blk, blk), pl.ds((i - 1) * blk, blk)] = -l_v[a + i - 1]
        for i in range(2, GROUP):
            width = (i - 1) * blk
            before = t_v[g, pl.ds((i - 1) * blk, blk), pl.ds(0, width)]
            t_v[g, pl.ds(i * blk, blk), pl.ds(0, width)] = (
                -dot(l_v[a + i - 1], before)
            ).astype(bf16)
        if g > 0:
            carry = -l_v[a - 1]
            cf_v[g, pl.ds(0, blk)] = carry
            for i in range(1, GROUP):
                carry = (-dot(l_v[a + i - 1], carry)).astype(bf16)
                cf_v[g, pl.ds(i * blk, blk)] = carry

    loads[2].wait()
    loads[3].wait()
    for k in range(nb - 1):
        e_v[k] = (-dot(d_v[k], u_v[k])).astype(bf16)

    pl.semaphore_wait(barrier, greeted)
    first = [
        face_copy(x_hbm.at[pl.ds(f * blk, blk)], nb0_v, 0, f) for f in range(faces)
    ]
    for c in reversed(first):
        c.start()

    for g in range(groups):
        a = g * GROUP
        for i in range(GROUP - 1, -1, -1):
            z_v[g, pl.ds(i * blk, blk), pl.ds(i * blk, blk)] = d_v[a + i]
            if i < GROUP - 1:
                width = (GROUP - 1 - i) * blk
                after = z_v[g, pl.ds((i + 1) * blk, blk), pl.ds((i + 1) * blk, width)]
                z_v[g, pl.ds(i * blk, blk), pl.ds((i + 1) * blk, width)] = dot(
                    e_v[a + i], after
                ).astype(bf16)
        if g < groups - 1:
            carry = e_v[a + GROUP - 1]
            cb_v[g, pl.ds((GROUP - 1) * blk, blk)] = carry
            for i in range(GROUP - 2, -1, -1):
                carry = dot(e_v[a + i], carry).astype(bf16)
                cb_v[g, pl.ds(i * blk, blk)] = carry

    loads[1].wait()
    for i in range(chunks):
        s_loads[i].wait()
        r0_v[pl.ds(i * rows, rows)] = -dot(s_v[pl.ds(i * rows, rows)], x_v[...])
    late[0].wait()
    late[1].wait()
    g00 = jnp.zeros((1, rhs), f32)
    for i in range(nb - 1, -1, -1):
        here = pl.ds(i * blk, blk)
        r = r0_v[here] + b_v[here].astype(f32)
        if i < faces:
            first[i ^ 1].wait_recv()
            r = r - dot(c_v[i], nb0_v[i])
        r0_v[here] = r
        g00 = g00 + colsum(r * r)

    gs = GROUP * blk

    def sweep_local(v_v, g):
        cat = split(v_v[pl.ds(g * gs, gs)])
        for i in range(GROUP):
            here = pl.ds(g * gs + i * blk, blk)
            w = v_v[here]
            if i > 0:
                w = w + fold(dot(t_v[g, pl.ds(i * blk, blk), pl.ds(0, i * blk)], cat[: i * blk]))
            w_v[here] = w

    def sweep_rest(z_out, finish):
        last = None
        for g in range(groups):
            rows_g = pl.ds(g * gs, gs)
            w = w_v[rows_g]
            if g > 0:
                w = w + fold(dot(cf_v[g], last))
            cat = split(w)
            wcat_v[rows_g] = cat
            last = cat[gs - blk :]
        head = None
        for g in range(groups - 1, -1, -1):
            for i in range(GROUP):
                b = g * GROUP + i
                rest = (GROUP - i) * blk
                z = fold(
                    dot(
                        z_v[g, pl.ds(i * blk, blk), pl.ds(i * blk, rest)],
                        wcat_v[pl.ds(b * blk, rest)],
                    )
                )
                if head is not None:
                    z = z + fold(dot(cb_v[g, pl.ds(i * blk, blk)], head))
                z_out[pl.ds(b * blk, blk)] = z
                finish(b, z)
                if i == 0:
                    following = split(z)
            head = following

    outside = pl.ds(fr, unknowns - fr)
    inside = pl.ds(0, fr)
    clear = -(-faces // GROUP)

    for g in range(groups):
        sweep_local(r0_v, g)
    second = {}

    def finish_first(b, z):
        cat = split(z)
        xcat_v[pl.ds(b * blk, blk)] = cat
        if b < faces:
            face_v[b] = cat[:, :rhs]
            second[b] = face_copy(face_v.at[b], nb1_v, 1, b)
            second[b].start()

    sweep_rest(d1_v, finish_first)
    g01 = jnp.zeros((1, rhs), f32)
    g11 = jnp.zeros((1, rhs), f32)
    m1_v[outside] = fold(dot(s_v[outside], xcat_v[...])) - r0_v[outside]
    for i in range(faces, nb):
        here = pl.ds(i * blk, blk)
        m = m1_v[here]
        g01 = g01 + colsum(m * r0_v[here])
        g11 = g11 + colsum(m * m)
    for g in range(clear, groups):
        sweep_local(m1_v, g)
    m1_v[inside] = fold(dot(s_v[inside], xcat_v[...])) - r0_v[inside]
    for i in range(faces - 1, -1, -1):
        here = pl.ds(i * blk, blk)
        second[i ^ 1].wait_recv()
        m = m1_v[here] + dot(c_v[i], nb1_v[i])
        m1_v[here] = m
        g01 = g01 + colsum(m * r0_v[here])
        g11 = g11 + colsum(m * m)

    starts = [0]
    for names in phases:
        starts.append(starts[-1] + math.prod(sizes[a] for a in names))

    def share(stage, p, total):
        names = phases[p]
        buf, at = sum_bufs[stage][p], place(names, me)
        buf[at] = total
        copies = [
            pltpu.make_async_remote_copy(
                src_ref=buf.at[at],
                dst_ref=buf.at[at],
                send_sem=sum_send.at[stage, starts[p] + k],
                recv_sem=sum_recv.at[stage, starts[p] + at],
                device_id=ids,
                device_id_type=MESH,
            )
            for k, ids in enumerate(peers(names))
        ]
        for c in copies:
            c.start()
        return copies

    def collect(stage, p, copies):
        names = phases[p]
        buf = sum_bufs[stage][p]
        for ids in peers(names):
            at = place(names, ids)
            pltpu.make_async_copy(
                buf.at[at], buf.at[at], sum_recv.at[stage, starts[p] + at]
            ).wait()
        terms = [buf[k] for k in range(buf.shape[0])]
        while len(terms) > 1:
            terms = [sum(terms[k : k + 2][1:], terms[k]) for k in range(0, len(terms), 2)]
        for c in copies:
            c.wait_send()
        return terms[0]

    early = share(0, 0, jnp.concatenate([g00, g01, g11], axis=0))

    for g in range(clear):
        sweep_local(m1_v, g)
    third = {}

    def finish_second(b, z):
        here = pl.ds(b * blk, blk)
        xd_v[here] = z.astype(bf16)
        if b < faces:
            third[b] = face_copy(xd_v.at[here], nb2_v, 2, b)
            third[b].start()

    sweep_rest(d2_v, finish_second)
    g02 = jnp.zeros((1, rhs), f32)
    g12 = jnp.zeros((1, rhs), f32)
    g22 = jnp.zeros((1, rhs), f32)
    w_v[outside] = dot(s_v[outside], xd_v[...])
    for i in range(faces, nb):
        here = pl.ds(i * blk, blk)
        m = w_v[here]
        g02 = g02 + colsum(m * r0_v[here])
        g12 = g12 + colsum(m * m1_v[here])
        g22 = g22 + colsum(m * m)
    w_v[inside] = dot(s_v[inside], xd_v[...])
    for i in range(faces - 1, -1, -1):
        here = pl.ds(i * blk, blk)
        third[i ^ 1].wait_recv()
        m = w_v[here] + dot(c_v[i], nb2_v[i])
        g02 = g02 + colsum(m * r0_v[here])
        g12 = g12 + colsum(m * m1_v[here])
        g22 = g22 + colsum(m * m)

    final = share(1, 0, jnp.concatenate([g02, g12, g22], axis=0))
    early_sum = collect(0, 0, early)
    final_sum = collect(1, 0, final)
    for p in range(1, len(phases)):
        early = share(0, p, early_sum)
        final = share(1, p, final_sum)
        early_sum = collect(0, p, early)
        final_sum = collect(1, p, final)
    zero = jnp.zeros((1, rhs), f32)
    g00, g01, g11 = [early_sum[i : i + 1] for i in range(3)]
    g02, g12, g22 = [final_sum[i : i + 1] for i in range(3)]
    b2 = g00 + EPS
    start = jnp.sqrt(b2)
    h00 = (g01 + g00) / b2
    de = h00 - 1.0
    n1 = (g11 - 2.0 * de * g01 + de * de * g00) / b2
    h10 = jnp.sqrt(jnp.maximum(n1, 0.0) + EPS)
    s2 = start * h10
    r0q = g02 - de * (g01 + g00)
    m1q = g12 - de * (g11 + g01)
    h01 = r0q / (start * s2)
    h11 = (m1q - de * r0q) / (s2 * s2)
    qq = (
        g22 - 2.0 * de * (g12 + g02) + de * de * (g11 + 2.0 * g01 + g00)
    ) / (s2 * s2)
    k00 = g00 / b2
    k11 = n1 / (h10 * h10)
    k01 = (g01 - de * g00) / (start * s2)
    n2 = qq - 2.0 * (h01 * h01 + h11 * h11) + h01 * h01 * k00 + h11 * h11 * k11
    n2 = n2 + 2.0 * h01 * h11 * k01
    h21 = jnp.sqrt(jnp.maximum(n2, 0.0) + EPS)
    c0, c1, ratio = least_squares([[h00, h01], [h10, h11], [zero, h21]], start)
    a2 = c1 / s2
    coef_ref[...] = jnp.concatenate([c0 / start - de * a2, a2], axis=0)
    ratio_ref[...] = ratio
    for f in range(faces):
        first[f].wait_send()
        second[f].wait_send()
        third[f].wait_send()


def combine(x_ref, d1_ref, d2_ref, coef_ref, ratio_ref, out_hbm, ratio_out, out_v, sem):
    chunks = sem.shape[0]
    rows = x_ref.shape[0] // chunks
    copies = []
    for i in range(chunks):
        here = pl.ds(i * rows, rows)
        out_v[here] = (
            x_ref[here].astype(f32)
            + coef_ref[0:1] * d1_ref[here]
            + coef_ref[1:2] * d2_ref[here]
        )
        copies.append(pltpu.make_async_copy(out_v.at[here], out_hbm.at[here], sem.at[i]))
        copies[-1].start()
    ratio_out[...] = ratio_ref[...]
    for c in copies:
        c.wait()


def body(sizes, loads, start_guess, schur, coupling, diag_inverse, lower, upper):
    b, x, s, c, d, l, u = [
        v.reshape(v.shape[3:])
        for v in (loads, start_guess, schur, coupling, diag_inverse, lower, upper)
    ]
    n, r = b.shape
    nb, blk = d.shape[:2]
    faces = c.shape[0]
    groups = nb // GROUP
    gs = GROUP * blk
    chunks = 4
    phases = (AXES,)
    if math.prod(sizes.values()) > 32:
        phases = (("gx",), ("gy",), ("gz",))
    counts = [math.prod(sizes[a] for a in names) for names in phases]
    hbm_spec = pl.BlockSpec(memory_space=pltpu.HBM)
    vmem = pl.BlockSpec(memory_space=pltpu.VMEM)
    x0, d1, d2, coef, ratio = pl.pallas_call(
        functools.partial(kernel, sizes, phases),
        out_shape=(
            pltpu.VMEM((n, r), bf16),
            pltpu.VMEM((n, r), f32),
            pltpu.VMEM((n, r), f32),
            pltpu.VMEM((2, r), f32),
            pltpu.VMEM((1, r), f32),
        ),
        in_specs=[hbm_spec] * 7,
        out_specs=(vmem,) * 5,
        scratch_shapes=[
            pltpu.VMEM(s.shape, bf16),
            pltpu.VMEM(c.shape, bf16),
            pltpu.VMEM(d.shape, bf16),
            pltpu.VMEM(l.shape, bf16),
            pltpu.VMEM(u.shape, bf16),
            pltpu.VMEM((n, r), bf16),
            pltpu.VMEM((n, r), bf16),
            pltpu.VMEM((groups, gs, gs), bf16),
            pltpu.VMEM((groups, gs, blk), bf16),
            pltpu.VMEM((nb - 1, blk, blk), bf16),
            pltpu.VMEM((groups, gs, gs), bf16),
            pltpu.VMEM((groups, gs, blk), bf16),
            pltpu.VMEM((n, r), f32),
            pltpu.VMEM((n, r), f32),
            pltpu.VMEM((n, r), f32),
            pltpu.VMEM((n, 2 * r), bf16),
            pltpu.VMEM((n, 2 * r), bf16),
            pltpu.VMEM((faces, blk, r), bf16),
            pltpu.VMEM((faces, blk, r), bf16),
            pltpu.VMEM((faces, blk, r), bf16),
            pltpu.VMEM((faces, blk, r), bf16),
            [[pltpu.VMEM((count, 3, r), f32) for count in counts] for _ in range(2)],
            pltpu.SemaphoreType.DMA((chunks,)),
            pltpu.SemaphoreType.DMA((6,)),
            pltpu.SemaphoreType.DMA((3, faces)),
            pltpu.SemaphoreType.DMA((3, faces)),
            pltpu.SemaphoreType.DMA((2, sum(counts))),
            pltpu.SemaphoreType.DMA((2, sum(counts))),
        ],
        compiler_params=pltpu.CompilerParams(
            collective_id=0, has_side_effects=True, vmem_limit_bytes=60 << 20
        ),
    )(b, x, s, c, d, l, u)
    out, ratio = pl.pallas_call(
        combine,
        out_shape=(jax.ShapeDtypeStruct((n, r), f32), jax.ShapeDtypeStruct((1, r), f32)),
        in_specs=[vmem] * 5,
        out_specs=(hbm_spec, vmem),
        scratch_shapes=[pltpu.VMEM((n, r), f32), pltpu.SemaphoreType.DMA((chunks,))],
        compiler_params=pltpu.CompilerParams(vmem_limit_bytes=8 << 20),
    )(x0, d1, d2, coef, ratio)
    return out[None, None, None], ratio.reshape(r)


def solution(mesh):
    sizes = {a: mesh.shape[a] for a in AXES}
    deep = P("gx", "gy", "gz", None, None, None)
    flat = P("gx", "gy", "gz", None, None)
    return jax.shard_map(
        functools.partial(body, sizes),
        mesh=mesh,
        in_specs=(flat, flat, flat, deep, deep, deep, deep),
        out_specs=(flat, P()),
        check_vma=False,
    )
```

```python
import functools
import itertools
import math

import jax
import jax.numpy as jnp
from jax import lax
from jax.experimental import pallas as pl
from jax.experimental.pallas import tpu as pltpu
from jax.sharding import PartitionSpec as P

AXES = ("gx", "gy", "gz")
MESH = pl.DeviceIdType.MESH
EPS = 1e-06
GROUP = 4
bf16 = jnp.bfloat16
f32 = jnp.float32


def dot(a, b):
    return jnp.dot(a, b, preferred_element_type=f32)


def split(v):
    hi = v.astype(bf16)
    lo = (v - hi.astype(f32)).astype(bf16)
    return jnp.concatenate([hi, lo], axis=1)


def fold(y):
    r = y.shape[1] // 2
    return y[:, :r] + y[:, r:]


def colsum(v):
    return jnp.sum(v, axis=0, keepdims=True)


def least_squares(h, start_norm):
    t00 = jnp.sqrt(h[0][0] * h[0][0] + h[1][0] * h[1][0])
    q0 = [h[0][0] / t00, h[1][0] / t00]
    t01 = q0[0] * h[0][1] + q0[1] * h[1][1]
    v1 = [h[0][1] - t01 * q0[0], h[1][1] - t01 * q0[1], h[2][1]]
    t11 = jnp.sqrt(v1[0] * v1[0] + v1[1] * v1[1] + v1[2] * v1[2])
    c1 = start_norm * (v1[0] / t11) / t11
    c0 = (start_norm * q0[0] - t01 * c1) / t00
    e0 = start_norm - h[0][0] * c0 - h[0][1] * c1
    e1 = h[1][0] * c0 + h[1][1] * c1
    e2 = h[2][1] * c1
    return c0, c1, jnp.sqrt(e0 * e0 + e1 * e1 + e2 * e2) / start_norm


def kernel(
    sizes, phases, b_hbm, x_hbm, s_hbm, c_hbm, d_hbm, l_hbm, u_hbm,
    x_v, d1_v, d2_v, coef_ref, ratio_ref,
    s_v, c_v, d_v, l_v, u_v, b_v, xd_v,
    t_v, cf_v, e_v, z_v, cb_v,
    r0_v, m1_v, w_v, wcat_v, xcat_v, face_v,
    nb0_v, nb1_v, nb2_v, sum_bufs,
    s_sem, in_sem, send_sem, recv_sem, sum_send, sum_recv,
):
    nb, blk = d_v.shape[0], d_v.shape[1]
    rhs = b_v.shape[1]
    unknowns = b_v.shape[0]
    faces = c_v.shape[0]
    groups = nb // GROUP
    chunks = s_sem.shape[0]
    rows = unknowns // chunks
    me = {a: lax.axis_index(a) for a in AXES}

    loads = [
        pltpu.make_async_copy(l_hbm, l_v, in_sem.at[0]),
        pltpu.make_async_copy(x_hbm, x_v, in_sem.at[1]),
        pltpu.make_async_copy(u_hbm, u_v, in_sem.at[2]),
        pltpu.make_async_copy(d_hbm, d_v, in_sem.at[3]),
    ]
    s_loads = [
        pltpu.make_async_copy(
            s_hbm.at[pl.ds(i * rows, rows)], s_v.at[pl.ds(i * rows, rows)], s_sem.at[i]
        )
        for i in range(chunks)
    ]
    late = [
        pltpu.make_async_copy(b_hbm, b_v, in_sem.at[4]),
        pltpu.make_async_copy(c_hbm, c_v, in_sem.at[5]),
    ]
    for c in loads + s_loads + late:
        c.start()

    away = {
        a: [me[a]] + [lax.rem(me[a] + k, sizes[a]) for k in range(1, sizes[a])] for a in AXES
    }

    def place(names, ids):
        index = 0
        for a in names:
            index = index * sizes[a] + ids[a]
        return index

    def peers(names):
        steps = itertools.product(*[range(sizes[a]) for a in names])
        return [
            {a: away[a][k] for a, k in zip(names, step)} for step in steps if any(step)
        ]

    barrier = pltpu.get_barrier_semaphore()
    greeted = 0
    for names in phases:
        for ids in peers(names):
            pl.semaphore_signal(barrier, inc=1, device_id=ids, device_id_type=MESH)
            greeted += 1

    def face_copy(src, dst, stage, f):
        a = AXES[f // 2]
        step = 1 if f % 2 else sizes[a] - 1
        return pltpu.make_async_remote_copy(
            src_ref=src,
            dst_ref=dst.at[f ^ 1],
            send_sem=send_sem.at[stage, f],
            recv_sem=recv_sem.at[stage, f ^ 1],
            device_id={a: lax.rem(me[a] + step, sizes[a])},
            device_id_type=MESH,
        )

    loads[0].wait()
    for g in range(groups):
        a = g * GROUP
        for i in range(1, GROUP):
            t_v[g, pl.ds(i * blk, blk), pl.ds((i - 1) * blk, blk)] = -l_v[a + i - 1]
        for i in range(2, GROUP):
            width = (i - 1) * blk
            before = t_v[g, pl.ds((i - 1) * blk, blk), pl.ds(0, width)]
            t_v[g, pl.ds(i * blk, blk), pl.ds(0, width)] = (
                -dot(l_v[a + i - 1], before)
            ).astype(bf16)
        if g > 0:
            carry = -l_v[a - 1]
            cf_v[g, pl.ds(0, blk)] = carry
            for i in range(1, GROUP):
                carry = (-dot(l_v[a + i - 1], carry)).astype(bf16)
                cf_v[g, pl.ds(i * blk, blk)] = carry

    loads[2].wait()
    loads[3].wait()
    for k in range(nb - 1):
        e_v[k] = (-dot(d_v[k], u_v[k])).astype(bf16)

    for g in range(groups):
        a = g * GROUP
        for i in range(GROUP - 1, -1, -1):
            z_v[g, pl.ds(i * blk, blk), pl.ds(i * blk, blk)] = d_v[a + i]
            if i < GROUP - 1:
                width = (GROUP - 1 - i) * blk
                after = z_v[g, pl.ds((i + 1) * blk, blk), pl.ds((i + 1) * blk, width)]
                z_v[g, pl.ds(i * blk, blk), pl.ds((i + 1) * blk, width)] = dot(
                    e_v[a + i], after
                ).astype(bf16)
        if g < groups - 1:
            carry = e_v[a + GROUP - 1]
            cb_v[g, pl.ds((GROUP - 1) * blk, blk)] = carry
            for i in range(GROUP - 2, -1, -1):
                carry = dot(e_v[a + i], carry).astype(bf16)
                cb_v[g, pl.ds(i * blk, blk)] = carry

    loads[1].wait()
    for i in range(chunks):
        s_loads[i].wait()
        r0_v[pl.ds(i * rows, rows)] = -dot(s_v[pl.ds(i * rows, rows)], x_v[...])
        if i == 0:
            pl.semaphore_wait(barrier, greeted)
            first = [
                face_copy(x_hbm.at[pl.ds(f * blk, blk)], nb0_v, 0, f) for f in range(faces)
            ]
            for c in reversed(first):
                c.start()
    late[0].wait()
    late[1].wait()
    g00 = jnp.zeros((1, rhs), f32)
    for i in range(nb - 1, -1, -1):
        here = pl.ds(i * blk, blk)
        r = r0_v[here] + b_v[here].astype(f32)
        if i < faces:
            first[i ^ 1].wait_recv()
            r = r - dot(c_v[i], nb0_v[i])
        r0_v[here] = r
        g00 = g00 + colsum(r * r)

    gs = GROUP * blk

    def sweep_local(v_v, g):
        cat = v_v[pl.ds(g * gs, gs)].astype(bf16)
        for i in range(GROUP):
            here = pl.ds(g * gs + i * blk, blk)
            w = v_v[here]
            if i > 0:
                w = w + dot(t_v[g, pl.ds(i * blk, blk), pl.ds(0, i * blk)], cat[: i * blk])
            w_v[here] = w

    def sweep_rest(z_out, finish):
        last = None
        for g in range(groups):
            rows_g = pl.ds(g * gs, gs)
            w = w_v[rows_g]
            if g > 0:
                w = w + dot(cf_v[g], last)
            cat = split(w)
            wcat_v[rows_g] = cat
            last = cat[gs - blk :, :rhs]
        head = None
        for g in range(groups - 1, -1, -1):
            for i in range(GROUP):
                b = g * GROUP + i
                rest = (GROUP - i) * blk
                z = fold(
                    dot(
                        z_v[g, pl.ds(i * blk, blk), pl.ds(i * blk, rest)],
                        wcat_v[pl.ds(b * blk, rest)],
                    )
                )
                if head is not None:
                    z = z + dot(cb_v[g, pl.ds(i * blk, blk)], head)
                z_out[pl.ds(b * blk, blk)] = z
                finish(b, z)
                if i == 0:
                    following = z.astype(bf16)
            head = following

    clear = -(-faces // GROUP)

    for g in range(groups):
        sweep_local(r0_v, g)
    second = {}

    def finish_first(b, z):
        cat = split(z)
        xcat_v[pl.ds(b * blk, blk)] = cat
        if b < faces:
            face_v[b] = cat[:, :rhs]
            second[b] = face_copy(face_v.at[b], nb1_v, 1, b)
            second[b].start()

    sweep_rest(d1_v, finish_first)
    g01 = jnp.zeros((1, rhs), f32)
    g11 = jnp.zeros((1, rhs), f32)
    m1_v[...] = fold(dot(s_v[...], xcat_v[...])) - r0_v[...]
    for i in range(faces, nb):
        here = pl.ds(i * blk, blk)
        m = m1_v[here]
        g01 = g01 + colsum(m * r0_v[here])
        g11 = g11 + colsum(m * m)
    for g in range(clear, groups):
        sweep_local(m1_v, g)
    for i in range(faces - 1, -1, -1):
        here = pl.ds(i * blk, blk)
        second[i ^ 1].wait_recv()
        m = m1_v[here] + dot(c_v[i], nb1_v[i])
        m1_v[here] = m
        g01 = g01 + colsum(m * r0_v[here])
        g11 = g11 + colsum(m * m)

    starts = [0]
    for names in phases:
        starts.append(starts[-1] + math.prod(sizes[a] for a in names))

    def share(stage, p, total):
        names = phases[p]
        buf, at = sum_bufs[stage][p], place(names, me)
        buf[at] = total
        copies = [
            pltpu.make_async_remote_copy(
                src_ref=buf.at[at],
                dst_ref=buf.at[at],
                send_sem=sum_send.at[stage, starts[p] + k],
                recv_sem=sum_recv.at[stage, starts[p] + at],
                device_id=ids,
                device_id_type=MESH,
            )
            for k, ids in enumerate(peers(names))
        ]
        for c in copies:
            c.start()
        return copies

    def collect(stage, p, copies):
        names = phases[p]
        buf = sum_bufs[stage][p]
        for ids in peers(names):
            at = place(names, ids)
            pltpu.make_async_copy(
                buf.at[at], buf.at[at], sum_recv.at[stage, starts[p] + at]
            ).wait()
        terms = [buf[k] for k in range(buf.shape[0])]
        while len(terms) > 1:
            terms = [sum(terms[k : k + 2][1:], terms[k]) for k in range(0, len(terms), 2)]
        for c in copies:
            c.wait_send()
        return terms[0]

    early = share(0, 0, jnp.concatenate([g00, g01, g11], axis=0))

    for g in range(clear):
        sweep_local(m1_v, g)
    third = {}

    def finish_second(b, z):
        here = pl.ds(b * blk, blk)
        xd_v[here] = z.astype(bf16)
        if b < faces:
            third[b] = face_copy(xd_v.at[here], nb2_v, 2, b)
            third[b].start()

    sweep_rest(d2_v, finish_second)
    g02 = jnp.zeros((1, rhs), f32)
    g12 = jnp.zeros((1, rhs), f32)
    g22 = jnp.zeros((1, rhs), f32)
    w_v[...] = dot(s_v[...], xd_v[...])
    for i in range(faces, nb):
        here = pl.ds(i * blk, blk)
        m = w_v[here]
        g02 = g02 + colsum(m * r0_v[here])
        g12 = g12 + colsum(m * m1_v[here])
        g22 = g22 + colsum(m * m)
    for i in range(faces - 1, -1, -1):
        here = pl.ds(i * blk, blk)
        third[i ^ 1].wait_recv()
        m = w_v[here] + dot(c_v[i], nb2_v[i])
        g02 = g02 + colsum(m * r0_v[here])
        g12 = g12 + colsum(m * m1_v[here])
        g22 = g22 + colsum(m * m)

    final = share(1, 0, jnp.concatenate([g02, g12, g22], axis=0))
    early_sum = collect(0, 0, early)
    final_sum = collect(1, 0, final)
    for p in range(1, len(phases)):
        early = share(0, p, early_sum)
        final = share(1, p, final_sum)
        early_sum = collect(0, p, early)
        final_sum = collect(1, p, final)
    zero = jnp.zeros((1, rhs), f32)
    g00, g01, g11 = [early_sum[i : i + 1] for i in range(3)]
    g02, g12, g22 = [final_sum[i : i + 1] for i in range(3)]
    b2 = g00 + EPS
    start = jnp.sqrt(b2)
    h00 = (g01 + g00) / b2
    de = h00 - 1.0
    n1 = (g11 - 2.0 * de * g01 + de * de * g00) / b2
    h10 = jnp.sqrt(jnp.maximum(n1, 0.0) + EPS)
    s2 = start * h10
    r0q = g02 - de * (g01 + g00)
    m1q = g12 - de * (g11 + g01)
    h01 = r0q / (start * s2)
    h11 = (m1q - de * r0q) / (s2 * s2)
    qq = (
        g22 - 2.0 * de * (g12 + g02) + de * de * (g11 + 2.0 * g01 + g00)
    ) / (s2 * s2)
    k00 = g00 / b2
    k11 = n1 / (h10 * h10)
    k01 = (g01 - de * g00) / (start * s2)
    n2 = qq - 2.0 * (h01 * h01 + h11 * h11) + h01 * h01 * k00 + h11 * h11 * k11
    n2 = n2 + 2.0 * h01 * h11 * k01
    h21 = jnp.sqrt(jnp.maximum(n2, 0.0) + EPS)
    c0, c1, ratio = least_squares([[h00, h01], [h10, h11], [zero, h21]], start)
    a2 = c1 / s2
    coef_ref[...] = jnp.concatenate([c0 / start - de * a2, a2], axis=0)
    ratio_ref[...] = ratio
    for f in range(faces):
        first[f].wait_send()
        second[f].wait_send()
        third[f].wait_send()


def combine(x_ref, d1_ref, d2_ref, coef_ref, ratio_ref, out_hbm, ratio_out, out_v, sem):
    chunks = sem.shape[0]
    rows = x_ref.shape[0] // chunks
    copies = []
    for i in range(chunks):
        here = pl.ds(i * rows, rows)
        out_v[here] = (
            x_ref[here].astype(f32)
            + coef_ref[0:1] * d1_ref[here]
            + coef_ref[1:2] * d2_ref[here]
        )
        copies.append(pltpu.make_async_copy(out_v.at[here], out_hbm.at[here], sem.at[i]))
        copies[-1].start()
    ratio_out[...] = ratio_ref[...]
    for c in copies:
        c.wait()


def body(sizes, loads, start_guess, schur, coupling, diag_inverse, lower, upper):
    b, x, s, c, d, l, u = [
        v.reshape(v.shape[3:])
        for v in (loads, start_guess, schur, coupling, diag_inverse, lower, upper)
    ]
    n, r = b.shape
    nb, blk = d.shape[:2]
    faces = c.shape[0]
    groups = nb // GROUP
    gs = GROUP * blk
    chunks = 4
    phases = (AXES,)
    if math.prod(sizes.values()) > 32:
        phases = (("gx",), ("gy",), ("gz",))
    counts = [math.prod(sizes[a] for a in names) for names in phases]
    hbm_spec = pl.BlockSpec(memory_space=pltpu.HBM)
    vmem = pl.BlockSpec(memory_space=pltpu.VMEM)
    x0, d1, d2, coef, ratio = pl.pallas_call(
        functools.partial(kernel, sizes, phases),
        out_shape=(
            pltpu.VMEM((n, r), bf16),
            pltpu.VMEM((n, r), f32),
            pltpu.VMEM((n, r), f32),
            pltpu.VMEM((2, r), f32),
            pltpu.VMEM((1, r), f32),
        ),
        in_specs=[hbm_spec] * 7,
        out_specs=(vmem,) * 5,
        scratch_shapes=[
            pltpu.VMEM(s.shape, bf16),
            pltpu.VMEM(c.shape, bf16),
            pltpu.VMEM(d.shape, bf16),
            pltpu.VMEM(l.shape, bf16),
            pltpu.VMEM(u.shape, bf16),
            pltpu.VMEM((n, r), bf16),
            pltpu.VMEM((n, r), bf16),
            pltpu.VMEM((groups, gs, gs), bf16),
            pltpu.VMEM((groups, gs, blk), bf16),
            pltpu.VMEM((nb - 1, blk, blk), bf16),
            pltpu.VMEM((groups, gs, gs), bf16),
            pltpu.VMEM((groups, gs, blk), bf16),
            pltpu.VMEM((n, r), f32),
            pltpu.VMEM((n, r), f32),
            pltpu.VMEM((n, r), f32),
            pltpu.VMEM((n, 2 * r), bf16),
            pltpu.VMEM((n, 2 * r), bf16),
            pltpu.VMEM((faces, blk, r), bf16),
            pltpu.VMEM((faces, blk, r), bf16),
            pltpu.VMEM((faces, blk, r), bf16),
            pltpu.VMEM((faces, blk, r), bf16),
            [[pltpu.VMEM((count, 3, r), f32) for count in counts] for _ in range(2)],
            pltpu.SemaphoreType.DMA((chunks,)),
            pltpu.SemaphoreType.DMA((6,)),
            pltpu.SemaphoreType.DMA((3, faces)),
            pltpu.SemaphoreType.DMA((3, faces)),
            pltpu.SemaphoreType.DMA((2, sum(counts))),
            pltpu.SemaphoreType.DMA((2, sum(counts))),
        ],
        compiler_params=pltpu.CompilerParams(
            collective_id=0, has_side_effects=True, vmem_limit_bytes=60 << 20
        ),
    )(b, x, s, c, d, l, u)
    out, ratio = pl.pallas_call(
        combine,
        out_shape=(jax.ShapeDtypeStruct((n, r), f32), jax.ShapeDtypeStruct((1, r), f32)),
        in_specs=[vmem] * 5,
        out_specs=(hbm_spec, vmem),
        scratch_shapes=[pltpu.VMEM((n, r), f32), pltpu.SemaphoreType.DMA((chunks,))],
        compiler_params=pltpu.CompilerParams(vmem_limit_bytes=8 << 20),
    )(x0, d1, d2, coef, ratio)
    return out[None, None, None], ratio.reshape(r)


def solution(mesh):
    sizes = {a: mesh.shape[a] for a in AXES}
    deep = P("gx", "gy", "gz", None, None, None)
    flat = P("gx", "gy", "gz", None, None)
    return jax.shard_map(
        functools.partial(body, sizes),
        mesh=mesh,
        in_specs=(flat, flat, flat, deep, deep, deep, deep),
        out_specs=(flat, P()),
        check_vma=False,
    )
```

```python
import functools
import itertools
import math

import jax
import jax.numpy as jnp
from jax import lax
from jax.experimental import pallas as pl
from jax.experimental.pallas import tpu as pltpu
from jax.sharding import PartitionSpec as P

AXES = ("gx", "gy", "gz")
MESH = pl.DeviceIdType.MESH
EPS = 1e-06
GROUP = 4
bf16 = jnp.bfloat16
f32 = jnp.float32


def dot(a, b):
    return jnp.dot(a, b, preferred_element_type=f32)


def split(v):
    hi = v.astype(bf16)
    lo = (v - hi.astype(f32)).astype(bf16)
    return jnp.concatenate([hi, lo], axis=1)


def fold(y):
    r = y.shape[1] // 2
    return y[:, :r] + y[:, r:]


def colsum(v):
    return jnp.sum(v, axis=0, keepdims=True)


def least_squares(h, start_norm):
    t00 = jnp.sqrt(h[0][0] * h[0][0] + h[1][0] * h[1][0])
    q0 = [h[0][0] / t00, h[1][0] / t00]
    t01 = q0[0] * h[0][1] + q0[1] * h[1][1]
    v1 = [h[0][1] - t01 * q0[0], h[1][1] - t01 * q0[1], h[2][1]]
    t11 = jnp.sqrt(v1[0] * v1[0] + v1[1] * v1[1] + v1[2] * v1[2])
    c1 = start_norm * (v1[0] / t11) / t11
    c0 = (start_norm * q0[0] - t01 * c1) / t00
    e0 = start_norm - h[0][0] * c0 - h[0][1] * c1
    e1 = h[1][0] * c0 + h[1][1] * c1
    e2 = h[2][1] * c1
    return c0, c1, jnp.sqrt(e0 * e0 + e1 * e1 + e2 * e2) / start_norm


def kernel(
    sizes, phases, b_hbm, x_hbm, s_hbm, c_hbm, d_hbm, l_hbm, u_hbm,
    x_v, d1_v, d2_v, coef_ref, ratio_ref,
    s_v, c_v, d_v, l_v, u_v, b_v, xd_v,
    t_v, cf_v, e_v, z_v, cb_v,
    r0_v, m1_v, w_v, wcat_v, xcat_v, face_v,
    nb0_v, nb1_v, nb2_v, sum_bufs,
    s_sem, in_sem, send_sem, recv_sem, sum_send, sum_recv,
):
    nb, blk = d_v.shape[0], d_v.shape[1]
    rhs = b_v.shape[1]
    unknowns = b_v.shape[0]
    faces = c_v.shape[0]
    groups = nb // GROUP
    chunks = s_sem.shape[0]
    rows = unknowns // chunks
    me = {a: lax.axis_index(a) for a in AXES}

    loads = [
        pltpu.make_async_copy(l_hbm, l_v, in_sem.at[0]),
        pltpu.make_async_copy(x_hbm, x_v, in_sem.at[1]),
        pltpu.make_async_copy(u_hbm, u_v, in_sem.at[2]),
        pltpu.make_async_copy(d_hbm, d_v, in_sem.at[3]),
    ]
    s_loads = [
        pltpu.make_async_copy(
            s_hbm.at[pl.ds(i * rows, rows)], s_v.at[pl.ds(i * rows, rows)], s_sem.at[i]
        )
        for i in range(chunks)
    ]
    late = [
        pltpu.make_async_copy(b_hbm, b_v, in_sem.at[4]),
        pltpu.make_async_copy(c_hbm, c_v, in_sem.at[5]),
    ]
    for c in loads + s_loads + late:
        c.start()

    away = {
        a: [me[a]] + [lax.rem(me[a] + k, sizes[a]) for k in range(1, sizes[a])] for a in AXES
    }

    def place(names, ids):
        index = 0
        for a in names:
            index = index * sizes[a] + ids[a]
        return index

    def peers(names):
        steps = itertools.product(*[range(sizes[a]) for a in names])
        return [
            {a: away[a][k] for a, k in zip(names, step)} for step in steps if any(step)
        ]

    barrier = pltpu.get_barrier_semaphore()
    greeted = 0
    for names in phases:
        for ids in peers(names):
            pl.semaphore_signal(barrier, inc=1, device_id=ids, device_id_type=MESH)
            greeted += 1

    def face_copy(src, dst, stage, f):
        a = AXES[f // 2]
        step = 1 if f % 2 else sizes[a] - 1
        return pltpu.make_async_remote_copy(
            src_ref=src,
            dst_ref=dst.at[f ^ 1],
            send_sem=send_sem.at[stage, f],
            recv_sem=recv_sem.at[stage, f ^ 1],
            device_id={a: lax.rem(me[a] + step, sizes[a])},
            device_id_type=MESH,
        )

    loads[0].wait()
    for g in range(groups):
        a = g * GROUP
        for i in range(1, GROUP):
            t_v[g, pl.ds(i * blk, blk), pl.ds((i - 1) * blk, blk)] = -l_v[a + i - 1]
        for i in range(2, GROUP):
            width = (i - 1) * blk
            before = t_v[g, pl.ds((i - 1) * blk, blk), pl.ds(0, width)]
            t_v[g, pl.ds(i * blk, blk), pl.ds(0, width)] = (
                -dot(l_v[a + i - 1], before)
            ).astype(bf16)
        if g > 0:
            carry = -l_v[a - 1]
            cf_v[g, pl.ds(0, blk)] = carry
            for i in range(1, GROUP):
                carry = (-dot(l_v[a + i - 1], carry)).astype(bf16)
                cf_v[g, pl.ds(i * blk, blk)] = carry

    loads[2].wait()
    loads[3].wait()
    for k in range(nb - 1):
        e_v[k] = (-dot(d_v[k], u_v[k])).astype(bf16)

    for g in range(groups):
        a = g * GROUP
        for i in range(GROUP - 1, -1, -1):
            z_v[g, pl.ds(i * blk, blk), pl.ds(i * blk, blk)] = d_v[a + i]
            if i < GROUP - 1:
                width = (GROUP - 1 - i) * blk
                after = z_v[g, pl.ds((i + 1) * blk, blk), pl.ds((i + 1) * blk, width)]
                z_v[g, pl.ds(i * blk, blk), pl.ds((i + 1) * blk, width)] = dot(
                    e_v[a + i], after
                ).astype(bf16)
        if g < groups - 1:
            carry = e_v[a + GROUP - 1]
            cb_v[g, pl.ds((GROUP - 1) * blk, blk)] = carry
            for i in range(GROUP - 2, -1, -1):
                carry = dot(e_v[a + i], carry).astype(bf16)
                cb_v[g, pl.ds(i * blk, blk)] = carry

    loads[1].wait()
    for i in range(chunks):
        s_loads[i].wait()
        r0_v[pl.ds(i * rows, rows)] = -dot(s_v[pl.ds(i * rows, rows)], x_v[...])
        if i == 0:
            pl.semaphore_wait(barrier, greeted)
            first = [
                face_copy(x_hbm.at[pl.ds(f * blk, blk)], nb0_v, 0, f) for f in range(faces)
            ]
            for c in reversed(first):
                c.start()
    late[0].wait()
    late[1].wait()
    g00 = jnp.zeros((1, rhs), f32)
    for i in range(nb - 1, -1, -1):
        here = pl.ds(i * blk, blk)
        r = r0_v[here] + b_v[here].astype(f32)
        if i < faces:
            first[i ^ 1].wait_recv()
            r = r - dot(c_v[i], nb0_v[i])
        r0_v[here] = r
        g00 = g00 + colsum(r * r)

    gs = GROUP * blk

    def sweep_local(v_v, g):
        cat = v_v[pl.ds(g * gs, gs)].astype(bf16)
        for i in range(GROUP):
            here = pl.ds(g * gs + i * blk, blk)
            w = v_v[here]
            if i > 0:
                w = w + dot(t_v[g, pl.ds(i * blk, blk), pl.ds(0, i * blk)], cat[: i * blk])
            w_v[here] = w

    def sweep_rest(z_out, finish):
        last = None
        for g in range(groups):
            rows_g = pl.ds(g * gs, gs)
            w = w_v[rows_g]
            if g > 0:
                w = w + dot(cf_v[g], last)
            cat = split(w)
            wcat_v[rows_g] = cat
            last = cat[gs - blk :, :rhs]
        head = None
        for g in range(groups - 1, -1, -1):
            for i in range(GROUP):
                b = g * GROUP + i
                rest = (GROUP - i) * blk
                z = fold(
                    dot(
                        z_v[g, pl.ds(i * blk, blk), pl.ds(i * blk, rest)],
                        wcat_v[pl.ds(b * blk, rest)],
                    )
                )
                if head is not None:
                    z = z + dot(cb_v[g, pl.ds(i * blk, blk)], head)
                z_out[pl.ds(b * blk, blk)] = z
                finish(b, z)
                if i == 0:
                    following = z.astype(bf16)
            head = following

    outside = pl.ds(faces * blk, unknowns - faces * blk)
    inside = pl.ds(0, faces * blk)
    clear = -(-faces // GROUP)

    for g in range(groups):
        sweep_local(r0_v, g)
    second = {}

    def finish_first(b, z):
        cat = split(z)
        xcat_v[pl.ds(b * blk, blk)] = cat
        if b < faces:
            face_v[b] = cat[:, :rhs]
            second[b] = face_copy(face_v.at[b], nb1_v, 1, b)
            second[b].start()

    sweep_rest(d1_v, finish_first)
    g01 = jnp.zeros((1, rhs), f32)
    g11 = jnp.zeros((1, rhs), f32)
    m1_v[outside] = fold(dot(s_v[outside], xcat_v[...])) - r0_v[outside]
    for i in range(faces, nb):
        here = pl.ds(i * blk, blk)
        m = m1_v[here]
        g01 = g01 + colsum(m * r0_v[here])
        g11 = g11 + colsum(m * m)
    for g in range(clear, groups):
        sweep_local(m1_v, g)
    m1_v[inside] = fold(dot(s_v[inside], xcat_v[...])) - r0_v[inside]
    for i in range(faces - 1, -1, -1):
        here = pl.ds(i * blk, blk)
        second[i ^ 1].wait_recv()
        m = m1_v[here] + dot(c_v[i], nb1_v[i])
        m1_v[here] = m
        g01 = g01 + colsum(m * r0_v[here])
        g11 = g11 + colsum(m * m)

    starts = [0]
    for names in phases:
        starts.append(starts[-1] + math.prod(sizes[a] for a in names))

    def share(stage, p, total):
        names = phases[p]
        buf, at = sum_bufs[stage][p], place(names, me)
        buf[at] = total
        copies = [
            pltpu.make_async_remote_copy(
                src_ref=buf.at[at],
                dst_ref=buf.at[at],
                send_sem=sum_send.at[stage, starts[p] + k],
                recv_sem=sum_recv.at[stage, starts[p] + at],
                device_id=ids,
                device_id_type=MESH,
            )
            for k, ids in enumerate(peers(names))
        ]
        for c in copies:
            c.start()
        return copies

    def collect(stage, p, copies):
        names = phases[p]
        buf = sum_bufs[stage][p]
        for ids in peers(names):
            at = place(names, ids)
            pltpu.make_async_copy(
                buf.at[at], buf.at[at], sum_recv.at[stage, starts[p] + at]
            ).wait()
        terms = [buf[k] for k in range(buf.shape[0])]
        while len(terms) > 1:
            terms = [sum(terms[k : k + 2][1:], terms[k]) for k in range(0, len(terms), 2)]
        for c in copies:
            c.wait_send()
        return terms[0]

    early = share(0, 0, jnp.concatenate([g00, g01, g11], axis=0))

    for g in range(clear):
        sweep_local(m1_v, g)
    third = {}

    def finish_second(b, z):
        here = pl.ds(b * blk, blk)
        xd_v[here] = z.astype(bf16)
        if b < faces:
            third[b] = face_copy(xd_v.at[here], nb2_v, 2, b)
            third[b].start()

    sweep_rest(d2_v, finish_second)
    g02 = jnp.zeros((1, rhs), f32)
    g12 = jnp.zeros((1, rhs), f32)
    g22 = jnp.zeros((1, rhs), f32)
    w_v[outside] = dot(s_v[outside], xd_v[...])
    for i in range(faces, nb):
        here = pl.ds(i * blk, blk)
        m = w_v[here]
        g02 = g02 + colsum(m * r0_v[here])
        g12 = g12 + colsum(m * m1_v[here])
        g22 = g22 + colsum(m * m)
    w_v[inside] = dot(s_v[inside], xd_v[...])
    for i in range(faces - 1, -1, -1):
        here = pl.ds(i * blk, blk)
        third[i ^ 1].wait_recv()
        m = w_v[here] + dot(c_v[i], nb2_v[i])
        g02 = g02 + colsum(m * r0_v[here])
        g12 = g12 + colsum(m * m1_v[here])
        g22 = g22 + colsum(m * m)

    final = share(1, 0, jnp.concatenate([g02, g12, g22], axis=0))
    early_sum = collect(0, 0, early)
    final_sum = collect(1, 0, final)
    for p in range(1, len(phases)):
        early = share(0, p, early_sum)
        final = share(1, p, final_sum)
        early_sum = collect(0, p, early)
        final_sum = collect(1, p, final)
    zero = jnp.zeros((1, rhs), f32)
    g00, g01, g11 = [early_sum[i : i + 1] for i in range(3)]
    g02, g12, g22 = [final_sum[i : i + 1] for i in range(3)]
    b2 = g00 + EPS
    start = jnp.sqrt(b2)
    h00 = (g01 + g00) / b2
    de = h00 - 1.0
    n1 = (g11 - 2.0 * de * g01 + de * de * g00) / b2
    h10 = jnp.sqrt(jnp.maximum(n1, 0.0) + EPS)
    s2 = start * h10
    r0q = g02 - de * (g01 + g00)
    m1q = g12 - de * (g11 + g01)
    h01 = r0q / (start * s2)
    h11 = (m1q - de * r0q) / (s2 * s2)
    qq = (
        g22 - 2.0 * de * (g12 + g02) + de * de * (g11 + 2.0 * g01 + g00)
    ) / (s2 * s2)
    k00 = g00 / b2
    k11 = n1 / (h10 * h10)
    k01 = (g01 - de * g00) / (start * s2)
    n2 = qq - 2.0 * (h01 * h01 + h11 * h11) + h01 * h01 * k00 + h11 * h11 * k11
    n2 = n2 + 2.0 * h01 * h11 * k01
    h21 = jnp.sqrt(jnp.maximum(n2, 0.0) + EPS)
    c0, c1, ratio = least_squares([[h00, h01], [h10, h11], [zero, h21]], start)
    a2 = c1 / s2
    coef_ref[...] = jnp.concatenate([c0 / start - de * a2, a2], axis=0)
    ratio_ref[...] = ratio
    for f in range(faces):
        first[f].wait_send()
        second[f].wait_send()
        third[f].wait_send()


def combine(x_ref, d1_ref, d2_ref, coef_ref, ratio_ref, out_hbm, ratio_out, out_v, sem):
    chunks = sem.shape[0]
    rows = x_ref.shape[0] // chunks
    copies = []
    for i in range(chunks):
        here = pl.ds(i * rows, rows)
        out_v[here] = (
            x_ref[here].astype(f32)
            + coef_ref[0:1] * d1_ref[here]
            + coef_ref[1:2] * d2_ref[here]
        )
        copies.append(pltpu.make_async_copy(out_v.at[here], out_hbm.at[here], sem.at[i]))
        copies[-1].start()
    ratio_out[...] = ratio_ref[...]
    for c in copies:
        c.wait()


def body(sizes, loads, start_guess, schur, coupling, diag_inverse, lower, upper):
    b, x, s, c, d, l, u = [
        v.reshape(v.shape[3:])
        for v in (loads, start_guess, schur, coupling, diag_inverse, lower, upper)
    ]
    n, r = b.shape
    nb, blk = d.shape[:2]
    faces = c.shape[0]
    groups = nb // GROUP
    gs = GROUP * blk
    chunks = 4
    phases = (AXES,)
    if math.prod(sizes.values()) > 32:
        phases = (("gx",), ("gy",), ("gz",))
    counts = [math.prod(sizes[a] for a in names) for names in phases]
    hbm_spec = pl.BlockSpec(memory_space=pltpu.HBM)
    vmem = pl.BlockSpec(memory_space=pltpu.VMEM)
    x0, d1, d2, coef, ratio = pl.pallas_call(
        functools.partial(kernel, sizes, phases),
        out_shape=(
            pltpu.VMEM((n, r), bf16),
            pltpu.VMEM((n, r), f32),
            pltpu.VMEM((n, r), f32),
            pltpu.VMEM((2, r), f32),
            pltpu.VMEM((1, r), f32),
        ),
        in_specs=[hbm_spec] * 7,
        out_specs=(vmem,) * 5,
        scratch_shapes=[
            pltpu.VMEM(s.shape, bf16),
            pltpu.VMEM(c.shape, bf16),
            pltpu.VMEM(d.shape, bf16),
            pltpu.VMEM(l.shape, bf16),
            pltpu.VMEM(u.shape, bf16),
            pltpu.VMEM((n, r), bf16),
            pltpu.VMEM((n, r), bf16),
            pltpu.VMEM((groups, gs, gs), bf16),
            pltpu.VMEM((groups, gs, blk), bf16),
            pltpu.VMEM((nb - 1, blk, blk), bf16),
            pltpu.VMEM((groups, gs, gs), bf16),
            pltpu.VMEM((groups, gs, blk), bf16),
            pltpu.VMEM((n, r), f32),
            pltpu.VMEM((n, r), f32),
            pltpu.VMEM((n, r), f32),
            pltpu.VMEM((n, 2 * r), bf16),
            pltpu.VMEM((n, 2 * r), bf16),
            pltpu.VMEM((faces, blk, r), bf16),
            pltpu.VMEM((faces, blk, r), bf16),
            pltpu.VMEM((faces, blk, r), bf16),
            pltpu.VMEM((faces, blk, r), bf16),
            [[pltpu.VMEM((count, 3, r), f32) for count in counts] for _ in range(2)],
            pltpu.SemaphoreType.DMA((chunks,)),
            pltpu.SemaphoreType.DMA((6,)),
            pltpu.SemaphoreType.DMA((3, faces)),
            pltpu.SemaphoreType.DMA((3, faces)),
            pltpu.SemaphoreType.DMA((2, sum(counts))),
            pltpu.SemaphoreType.DMA((2, sum(counts))),
        ],
        compiler_params=pltpu.CompilerParams(
            collective_id=0, has_side_effects=True, vmem_limit_bytes=60 << 20
        ),
    )(b, x, s, c, d, l, u)
    out, ratio = pl.pallas_call(
        combine,
        out_shape=(jax.ShapeDtypeStruct((n, r), f32), jax.ShapeDtypeStruct((1, r), f32)),
        in_specs=[vmem] * 5,
        out_specs=(hbm_spec, vmem),
        scratch_shapes=[pltpu.VMEM((n, r), f32), pltpu.SemaphoreType.DMA((chunks,))],
        compiler_params=pltpu.CompilerParams(vmem_limit_bytes=8 << 20),
    )(x0, d1, d2, coef, ratio)
    return out[None, None, None], ratio.reshape(r)


def solution(mesh):
    sizes = {a: mesh.shape[a] for a in AXES}
    deep = P("gx", "gy", "gz", None, None, None)
    flat = P("gx", "gy", "gz", None, None)
    return jax.shard_map(
        functools.partial(body, sizes),
        mesh=mesh,
        in_specs=(flat, flat, flat, deep, deep, deep, deep),
        out_specs=(flat, P()),
        check_vma=False,
    )
```
